32 devices in a mesh: depth: 8 (over y, x, core), dp: 4 (over z).
Axes of the slice: x: 2, y: 2, z: 4, core: 2. Of those that a mesh axis runs over, the one named last changes fastest.
Arguments:
- token_ids: int32 [512], P('dp'), may hold values from 0 to 10239
- embedding: bfloat16 [10240, 512], P('depth'), may hold values from -6 to 6
- w_up: bfloat16 [16, 512, 2048], P('depth'), may hold values from -0.25 to 0.25
- w_down: bfloat16 [16, 2048, 512], P('depth'), may hold values from -0.125 to 0.125
- cotangent: bfloat16 [512, 512], P('dp'), may hold values from -0.119628906 to 0.119628906
Outputs:
- grad_up: float32 [16, 512, 2048], P('depth', 'dp')
- grad_down: float32 [16, 2048, 512], P('depth', 'dp')
The draws below stay inside these ranges and needn't reach their ends.
All inputs are finite; a program needn't handle non-finite values.
Results may differ from the reference program's by a relative error of at most 0.03.
Values may be sent and summed in bfloat16 or wider, within the bound.
No kernel may reach another device: no remote copies, remote signals or barrier semaphores. Data moves between devices by JAX's collectives and lax.ppermute only.
A program may use at most 64 MiB of HBM per device.

```python
import jax
import jax.numpy as jnp
from jax import lax

D = 512
FF = 2048
L_DEV = 2
RELAX = 3
LAYERS = 16
VOCAB = 10240
TOKENS = 512
N_DEPTH = 8


def set_ends(entries, rng, least, high):
    place = [jax.random.randint(jax.random.fold_in(rng, axis), (), 0, length) for axis, length in enumerate(entries.shape)]
    longest = entries.shape.index(max(entries.shape))
    next_to = place[:longest] + [(place[longest] + 1) % entries.shape[longest]] + place[longest + 1:]
    return entries.at[tuple(place)].set(least).at[tuple(next_to)].set(high)


def shard_levels(own_key, dims, pieces, low, top_value):
    loudness, own = 1.0, jax.random.fold_in(own_key, 6)
    for dim, parts in pieces:
        draws = jnp.exp(jax.random.uniform(jax.random.fold_in(own, dim), (parts,), jnp.float32, low / len(pieces), top_value / len(pieces)))
        loudness = loudness * jnp.repeat(draws, dims[dim] // parts).reshape([-1 if axis == dim else 1 for axis in range(len(dims))])
    return loudness


def normal_values(key, dims, width, reach, split=(), kind=jnp.bfloat16):
    values = jax.random.normal(key, dims, jnp.float32) * width
    if len(split) > 0:
        values = shard_levels(key, dims, split, -0.22, 0.18) * values
    return jnp.clip(values, min=-reach, max=reach).astype(kind)


def setup_inputs(seed: int = 0) -> dict:
    streams_of = jax.random.split(jax.random.key(seed), 6)
    token_ids = set_ends(jax.random.randint(streams_of[0], (TOKENS,), 0, VOCAB), jax.random.fold_in(streams_of[0], 1), 0, VOCAB - 1).astype(jnp.int32)
    embedding = normal_values(streams_of[1], (VOCAB, D), 1.0, 6.0, ((0, 8),))
    w_up = normal_values(streams_of[2], (LAYERS, D, FF), D ** -0.5, 0.25, ((0, 8),))
    w_down = normal_values(streams_of[3], (LAYERS, FF, D), FF ** -0.5, 0.125, ((0, 8),))
    cotangent = normal_values(streams_of[4], (TOKENS, D), 0.02, 0.119628906, ((0, 4),))
    return {"token_ids": token_ids, "embedding": embedding, "w_up": w_up, "w_down": w_down, "cotangent": cotangent}


EPSILON = 1e-06
GAMMA = 0.05

def layer_forward(state, weight_up, weight_down):
    scale = lax.rsqrt(lax.optimization_barrier(jnp.mean(state * state, axis=-1, keepdims=True)) + EPSILON)
    normed = (state * scale).astype(jnp.bfloat16)
    before = jnp.dot(normed, weight_up, preferred_element_type=jnp.float32)
    hidden = jax.nn.silu(before).astype(jnp.bfloat16)
    output = state + jnp.dot(hidden, weight_down, preferred_element_type=jnp.float32)
    return (output, (scale, normed, before, hidden))

def layer_adjoint(state, saved, adjoint, weight_up, weight_down):
    scale, normed, before, hidden = saved
    adjoint_low = adjoint.astype(jnp.bfloat16)
    toward_hidden = lax.dot_general(adjoint_low, weight_down, (((1,), (1,)), ((), ())), preferred_element_type=jnp.float32)
    sigma = jax.nn.sigmoid(before)
    delta = (toward_hidden * sigma * (1.0 + before * (1.0 - sigma))).astype(jnp.bfloat16)
    toward_normed = lax.dot_general(delta, weight_up, (((1,), (1,)), ((), ())), preferred_element_type=jnp.float32)
    unit = state * scale
    inner = lax.optimization_barrier(jnp.mean(toward_normed * unit, axis=-1, keepdims=True))
    return (adjoint + scale * (toward_normed - unit * inner), adjoint_low, delta)

def coarse_matrix(weight_up, weight_down):
    total = jnp.dot(weight_up[0], weight_down[0], preferred_element_type=jnp.float32)
    for layer in range(1, weight_up.shape[0]):
        total = total + jnp.dot(weight_up[layer], weight_down[layer], preferred_element_type=jnp.float32)
    return jnp.eye(weight_up.shape[1], dtype=jnp.float32) + GAMMA * total

def block_forward(packed):
    state, ups, downs = packed
    for layer in range(L_DEV):
        state, unused = layer_forward(state, ups[layer], downs[layer])
    return state

def block_states(packed):
    state, ups, downs = packed
    inputs = []
    for layer in range(L_DEV):
        inputs.append(state)
        state, unused = layer_forward(state, ups[layer], downs[layer])
    return jnp.stack(inputs, 0)

def block_adjoint(packed):
    adjoint, states, ups, downs = packed
    for layer in reversed(range(L_DEV)):
        unused, saved = layer_forward(states[layer], ups[layer], downs[layer])
        adjoint, low, delta = layer_adjoint(states[layer], saved, adjoint, ups[layer], downs[layer])
    return adjoint

def block_grads(packed):
    adjoint, states, ups, downs = packed
    grads_up = [None] * L_DEV
    grads_down = [None] * L_DEV
    for layer in reversed(range(L_DEV)):
        unused, saved = layer_forward(states[layer], ups[layer], downs[layer])
        scale, normed, before, hidden = saved
        adjoint, low, delta = layer_adjoint(states[layer], saved, adjoint, ups[layer], downs[layer])
        grads_down[layer] = lax.dot_general(hidden, low, (((0,), (0,)), ((), ())), preferred_element_type=jnp.float32)
        grads_up[layer] = lax.dot_general(normed, delta, (((0,), (0,)), ((), ())), preferred_element_type=jnp.float32)
    return (jnp.stack(grads_up, 0), jnp.stack(grads_down, 0))

def project(packed):
    return jnp.dot(packed[0], packed[1], precision=lax.Precision.HIGHEST)

def forward_link(carry, packed):
    matrix, rest = packed
    carry = jnp.dot(carry, matrix, precision=lax.Precision.HIGHEST) + rest
    return (carry, carry)

def reference(token_ids, embedding, w_up, w_down, cotangent):
    start = jnp.take(embedding, token_ids, axis=0).astype(jnp.float32)
    ups = w_up.reshape(N_DEPTH, L_DEV, D, FF)
    downs = w_down.reshape(N_DEPTH, L_DEV, FF, D)
    matrices = lax.map(lambda packed: coarse_matrix(packed[0], packed[1]), (ups, downs))
    transposed = jnp.swapaxes(matrices, 1, 2)
    zeros = jnp.zeros_like(start)
    coarse = jnp.broadcast_to(start[None], (N_DEPTH,) + start.shape)
    previous = coarse
    for sweep in range(RELAX):
        ends = lax.map(block_forward, (coarse, ups, downs))
        previous = coarse
        coarse = jnp.concatenate([start[None], ends[:-1]], 0)
    projected = lax.map(project, (previous, matrices))
    tau = coarse - jnp.concatenate([zeros[None], projected[:-1]], 0)
    unused, carried = lax.scan(forward_link, tau[0], (matrices[:-1], tau[1:]))
    corrected = jnp.concatenate([tau[:1], carried], 0)
    states = lax.map(block_states, (corrected, ups, downs))
    final = cotangent.astype(jnp.float32)
    adjoints = jnp.broadcast_to(final[None], (N_DEPTH,) + final.shape)
    before = adjoints
    for sweep in range(RELAX):
        begins = lax.map(block_adjoint, (adjoints, states, ups, downs))
        before = adjoints
        adjoints = jnp.concatenate([begins[1:], final[None]], 0)
    back_projected = lax.map(project, (before, transposed))
    back_tau = adjoints - jnp.concatenate([back_projected[1:], zeros[None]], 0)
    unused, back_carried = lax.scan(forward_link, back_tau[-1], (transposed[1:], back_tau[:-1]), reverse=True)
    adjoint_corrected = jnp.concatenate([back_carried, back_tau[-1:]], 0)
    grad_up, grad_down = lax.map(block_grads, (adjoint_corrected, states, ups, downs))
    return (grad_up.reshape(N_DEPTH * L_DEV, D, FF), grad_down.reshape(N_DEPTH * L_DEV, FF, D))
```

```python
import jax
import jax.numpy as jnp
from jax import lax
from jax.sharding import PartitionSpec as P

RELAX = 3


EPSILON = 1e-06
GAMMA = 0.05
CHUNK = 512


def swapped(block, axis, mask):
    devices = range(lax.axis_size(axis))
    return lax.ppermute(block, axis, [(i, i ^ mask) for i in devices])


def rotated(block, axis, distance):
    size = lax.axis_size(axis)
    return lax.ppermute(block, axis, [(i, (i + distance) % size) for i in range(size)])


def times(left, right):
    return jnp.dot(
        left.astype(jnp.bfloat16), right.astype(jnp.bfloat16), preferred_element_type=jnp.float32
    )


def times_transposed(left, right):
    return lax.dot_general(
        left.astype(jnp.bfloat16),
        right.astype(jnp.bfloat16),
        (((1,), (1,)), ((), ())),
        preferred_element_type=jnp.float32,
    )


def layer_forward(state, weight_up, weight_down):
    scale = lax.rsqrt(jnp.mean(state * state, axis=-1, keepdims=True) + EPSILON)
    normed = (state * scale).astype(jnp.bfloat16)
    before = jnp.dot(normed, weight_up, preferred_element_type=jnp.float32)
    hidden = jax.nn.silu(before).astype(jnp.bfloat16)
    output = state + jnp.dot(hidden, weight_down, preferred_element_type=jnp.float32)
    return (output, (scale, normed, before, hidden))


def layer_adjoint(state, saved, adjoint, weight_up, weight_down):
    scale, normed, before, hidden = saved
    adjoint_low = adjoint.astype(jnp.bfloat16)
    toward_hidden = times_transposed(adjoint_low, weight_down)
    sigma = jax.nn.sigmoid(before)
    delta = (toward_hidden * sigma * (1.0 + before * (1.0 - sigma))).astype(jnp.bfloat16)
    toward_normed = times_transposed(delta, weight_up)
    unit = state * scale
    inner = jnp.mean(toward_normed * unit, axis=-1, keepdims=True)
    return (adjoint + scale * (toward_normed - unit * inner), adjoint_low, delta)


def coarse_part(w_up, w_down):
    total = jnp.dot(w_up[0], w_down[0], preferred_element_type=jnp.float32)
    for layer in range(1, w_up.shape[0]):
        total = total + jnp.dot(w_up[layer], w_down[layer], preferred_element_type=jnp.float32)
    return GAMMA * total


def joined(left, right):
    return left + right + times(left, right)


def matrix_scan(own, position, bits):
    whole = own
    prefix = jnp.zeros_like(own)
    suffix = jnp.zeros_like(own)
    steps = []
    for bit in range(bits):
        upper = ((position >> bit) & 1) == 1
        low = high = None
        if bit < bits - 1:
            other = swapped(whole.astype(jnp.bfloat16), "depth", 1 << bit).astype(jnp.float32)
            low = jnp.where(upper, other, whole)
            high = jnp.where(upper, whole, other)
        steps.append((prefix, suffix, low, high))
        if bit < bits - 1:
            prefix = jnp.where(upper, joined(low, prefix), prefix)
            suffix = jnp.where(upper, suffix, joined(suffix, high))
            if bit < bits - 2:
                whole = joined(low, high)
    return steps


def gathered(block, axis):
    size = lax.axis_size(axis)
    index = lax.axis_index(axis)
    rows = block.shape[0]
    whole = jnp.zeros((size * rows,) + block.shape[1:], block.dtype)
    for distance in range(size):
        piece = rotated(block, axis, distance) if distance else block
        source = lax.rem(index + size - distance, size)
        whole = lax.dynamic_update_slice_in_dim(whole, piece, source * rows, 0)
    return whole


def shards(token_ids, embedding, w_up, w_down, cotangent):
    depth = lax.axis_size("depth")
    bits = depth.bit_length() - 1
    assert depth == 1 << bits
    position = lax.axis_index("depth")
    first = position == 0
    final_block = position == depth - 1
    layers = w_up.shape[0]
    vocab_rows = embedding.shape[0]
    local_ids = token_ids - position * vocab_rows
    inside = (local_ids >= 0) & (local_ids < vocab_rows)
    picked = jnp.take(embedding, jnp.clip(local_ids, 0, vocab_rows - 1), axis=0)
    picked = jnp.where(inside[:, None], picked, jnp.zeros_like(picked))
    picked = picked + swapped(picked, "depth", 1)
    arrivals = [swapped(picked, "depth", mask) for mask in range(2, depth, 2)]
    for arrival in arrivals:
        picked = picked + arrival
    start = picked.astype(jnp.float32)
    own = coarse_part(w_up, w_down)
    steps = matrix_scan(own, position, bits)

    def run_forward(state):
        for layer in range(layers):
            state, unused = layer_forward(state, w_up[layer], w_down[layer])
        return state

    coarse = start
    for sweep in range(RELAX - 1):
        arrived = rotated(run_forward(coarse).astype(jnp.bfloat16), "depth", 1)
        coarse = jnp.where(first, start, arrived.astype(jnp.float32))
    ended = run_forward(coarse)
    value = jnp.where(first, ended, ended - coarse - times(coarse, own))
    corrected = jnp.zeros_like(start)
    for bit in range(bits):
        prefix, suffix, low, high = steps[bit]
        upper = ((position >> bit) & 1) == 1
        other = swapped(value.astype(jnp.bfloat16), "depth", 1 << bit).astype(jnp.float32)
        lower_value = jnp.where(upper, other, value)
        corrected = corrected + jnp.where(upper, lower_value + times(lower_value, prefix), 0.0)
        if bit < bits - 1:
            upper_value = jnp.where(upper, value, other)
            value = upper_value + lower_value + times(lower_value, high)
    corrected = jnp.where(first, start, corrected)
    corrected_low = corrected.astype(jnp.bfloat16)
    corrected = corrected_low.astype(jnp.float32)

    def block_saves(state):
        states = []
        saves = []
        for layer in range(layers):
            states.append(state)
            state, saved = layer_forward(state, w_up[layer], w_down[layer])
            saves.append(saved)
        return states, saves

    states, saves = block_saves(corrected)

    def run_adjoint(adjoint):
        for layer in reversed(range(layers)):
            adjoint, low, delta = layer_adjoint(
                states[layer], saves[layer], adjoint, w_up[layer], w_down[layer]
            )
        return adjoint

    final = cotangent.astype(jnp.float32)
    adjoint_state = final
    for sweep in range(RELAX - 1):
        arrived = rotated(run_adjoint(adjoint_state).astype(jnp.bfloat16), "depth", -1)
        adjoint_state = jnp.where(final_block, final, arrived.astype(jnp.float32))
    begun = run_adjoint(adjoint_state)
    value = jnp.where(
        final_block, begun, begun - adjoint_state - times_transposed(adjoint_state, own)
    )
    adjoint = jnp.zeros_like(final)
    for bit in range(bits):
        prefix, suffix, low, high = steps[bit]
        upper = ((position >> bit) & 1) == 1
        other = swapped(value.astype(jnp.bfloat16), "depth", 1 << bit).astype(jnp.float32)
        upper_value = jnp.where(upper, value, other)
        adjoint = adjoint + jnp.where(
            upper, 0.0, upper_value + times_transposed(upper_value, suffix)
        )
        if bit < bits - 1:
            lower_value = jnp.where(upper, other, value)
            value = lower_value + upper_value + times_transposed(upper_value, low)
    adjoint = jnp.where(final_block, final, adjoint)

    parts = lax.axis_size("dp")
    part = lax.axis_index("dp")

    def own_columns(block):
        width = block.shape[1] // parts
        return lax.dynamic_slice_in_dim(block, part * width, width, 1)

    def over_tokens(left, right):
        return lax.dot_general(
            left, right, (((0,), (0,)), ((), ())), preferred_element_type=jnp.float32
        )

    def chunk_grads(state_low, adjoint_low):
        inputs, saves = block_saves(state_low.astype(jnp.float32))
        adjoint = adjoint_low.astype(jnp.float32)
        grads_up = [None] * layers
        grads_down = [None] * layers
        for layer in reversed(range(layers)):
            scale, normed, before, hidden = saves[layer]
            adjoint, low, delta = layer_adjoint(
                inputs[layer], saves[layer], adjoint, w_up[layer], w_down[layer]
            )
            grads_down[layer] = over_tokens(own_columns(hidden), low)
            grads_up[layer] = over_tokens(own_columns(normed), delta)
        return (jnp.stack(grads_up, 0), jnp.stack(grads_down, 0))

    all_corrected = gathered(corrected_low, "dp")
    all_adjoint = gathered(adjoint.astype(jnp.bfloat16), "dp")
    tokens = all_corrected.shape[0]
    chunk = min(tokens, CHUNK)
    if tokens == chunk:
        return chunk_grads(all_corrected, all_adjoint)

    def add_chunk(turn, grads):
        rows = lambda block: lax.dynamic_slice_in_dim(block, turn * chunk, chunk, 0)
        more = chunk_grads(rows(all_corrected), rows(all_adjoint))
        return (grads[0] + more[0], grads[1] + more[1])

    shapes = jax.eval_shape(chunk_grads, all_corrected[:chunk], all_adjoint[:chunk])
    zeros = tuple(jnp.zeros(shape.shape, shape.dtype) for shape in shapes)
    return lax.fori_loop(0, tokens // chunk, add_chunk, zeros)


def solution(mesh):
    in_specs = (
        P("dp"),
        P("depth", None),
        P("depth", None, None),
        P("depth", None, None),
        P("dp", None),
    )
    out_specs = (P("depth", "dp", None), P("depth", "dp", None))
    return jax.shard_map(shards, mesh=mesh, in_specs=in_specs, out_specs=out_specs, check_vma=False)
```

```python
import functools

import jax
import jax.numpy as jnp
from jax import lax
from jax.experimental import pallas as pl
from jax.experimental.pallas import tpu as pltpu
from jax.sharding import PartitionSpec as P

RELAX = 3


EPSILON = 1e-06
GAMMA = 0.05
CHUNK = 512
MIB = 1 << 20

LOW = jnp.bfloat16
FULL = jnp.float32


def swapped(block, axis, mask):
    devices = range(lax.axis_size(axis))
    return lax.ppermute(block, axis, [(i, i ^ mask) for i in devices])


def rotated(block, axis, distance):
    size = lax.axis_size(axis)
    return lax.ppermute(block, axis, [(i, (i + distance) % size) for i in range(size)])


def dot(left, right):
    return jnp.dot(left.astype(LOW), right.astype(LOW), preferred_element_type=FULL)


def dot_transposed(left, right):
    return lax.dot_general(
        left.astype(LOW), right.astype(LOW), (((1,), (1,)), ((), ())), preferred_element_type=FULL
    )


def call(body, name, flops, limit, out_shapes, position, *args):
    whole = pl.BlockSpec(memory_space=pltpu.VMEM)
    moved = sum(a.size * a.dtype.itemsize for a in args)
    return pl.pallas_call(
        body,
        out_shape=out_shapes,
        in_specs=[pl.BlockSpec(memory_space=pltpu.SMEM)] + [whole] * len(args),
        out_specs=jax.tree.map(lambda unused: whole, out_shapes),
        name=name,
        compiler_params=pltpu.CompilerParams(vmem_limit_bytes=limit * MIB),
        cost_estimate=pl.CostEstimate(flops=flops, bytes_accessed=moved // 4, transcendentals=0),
    )(position, *args)


def shape(dims, kind):
    return jax.ShapeDtypeStruct(dims, kind)


def row_scale(state):
    return lax.rsqrt(jnp.mean(state * state, axis=-1, keepdims=True) + EPSILON)


def block_forward(state, up_ref, down_ref):
    for layer in range(up_ref.shape[0]):
        normed = (state * row_scale(state)).astype(LOW)
        before = dot(normed, up_ref[layer])
        hidden = (before / (1.0 + jnp.exp(-before))).astype(LOW)
        state = state + dot(hidden, down_ref[layer])
    return state


def block_adjoint(adjoint, slope_ref, unit_ref, scale_ref, up_ref, down_ref):
    for layer in reversed(range(up_ref.shape[0])):
        toward_hidden = dot_transposed(adjoint, down_ref[layer])
        delta = (toward_hidden * slope_ref[layer]).astype(LOW)
        toward_normed = dot_transposed(delta, up_ref[layer])
        unit = unit_ref[layer]
        inner = jnp.mean(toward_normed * unit, axis=-1, keepdims=True)
        adjoint = adjoint + scale_ref[layer] * (toward_normed - unit * inner)
    return adjoint


def save_forward(state, up_ref, down_ref, slope_ref, unit_ref, scale_ref, normed_ref, hidden_ref):
    layers = up_ref.shape[0]
    for layer in range(layers):
        scale = row_scale(state)
        unit = state * scale
        normed = unit.astype(LOW)
        before = dot(normed, up_ref[layer])
        sigma = 1.0 / (1.0 + jnp.exp(-before))
        slope_ref[layer] = sigma * (1.0 + before * (1.0 - sigma))
        unit_ref[layer] = unit
        scale_ref[layer] = scale
        if normed_ref is not None:
            normed_ref[layer] = normed
        if hidden_ref is not None or layer < layers - 1:
            hidden = (before * sigma).astype(LOW)
            if hidden_ref is not None:
                hidden_ref[layer] = hidden
            if layer < layers - 1:
                state = state + dot(hidden, down_ref[layer])


def coarse_kernel(position_ref, up_ref, down_ref, out_ref):
    total = dot(up_ref[0], down_ref[0])
    for layer in range(1, up_ref.shape[0]):
        total = total + dot(up_ref[layer], down_ref[layer])
    out_ref[...] = (GAMMA * total).astype(LOW)


def joined(left, right):
    return left.astype(FULL) + right.astype(FULL) + dot(left, right)


def join_kernel(bit, last, position_ref, whole_ref, other_ref, *refs):
    upper = ((position_ref[0] >> bit) & 1) == 1
    whole, other = whole_ref[...], other_ref[...]
    low = jnp.where(upper, other, whole)
    high = jnp.where(upper, whole, other)
    refs = list(refs)
    zeros = jnp.zeros_like(low)
    if bit > 0:
        before, after = refs.pop(0)[...], refs.pop(0)[...]
        prefix = jnp.where(upper, joined(low, before).astype(LOW), before)
        suffix = jnp.where(upper, after, joined(after, high).astype(LOW))
    else:
        prefix = jnp.where(upper, low, zeros)
        suffix = jnp.where(upper, zeros, high)
    refs[0][...] = low
    refs[1][...] = high
    refs[2][...] = prefix
    refs[3][...] = suffix
    if not last:
        refs[4][...] = joined(low, high).astype(LOW)


def matrix_scan(own, position, bits):
    width = own.shape[0]
    square = shape(own.shape, LOW)
    whole, prefix, suffix = own, None, None
    steps = []
    for bit in range(bits - 1):
        last = bit == bits - 2
        other = swapped(whole, "depth", 1 << bit)
        args = (whole, other) if bit == 0 else (whole, other, prefix, suffix)
        outs = call(
            functools.partial(join_kernel, bit, last),
            f"join_{bit}",
            6 * width**3,
            12,
            [square] * (4 if last else 5),
            position,
            *args,
        )
        steps.append((prefix, suffix, outs[0], outs[1]))
        prefix, suffix = outs[2], outs[3]
        whole = None if last else outs[4]
    steps.append((prefix, suffix, None, None))
    return steps


def scan_values(forward, bit, position_ref, value_ref, other_ref):
    upper = ((position_ref[0] >> bit) & 1) == 1
    value, other = value_ref[...].astype(FULL), other_ref[...].astype(FULL)
    lower_value = jnp.where(upper, other, value)
    upper_value = jnp.where(upper, value, other)
    if forward:
        return upper, lower_value, upper_value
    return jnp.logical_not(upper), upper_value, lower_value


def scan_kernel(forward, bit, position_ref, value_ref, other_ref, matrix_ref, *refs):
    receives, donor, keep = scan_values(forward, bit, position_ref, value_ref, other_ref)
    times = dot if forward else dot_transposed
    if bit == 0:
        out_ref, next_ref = refs
        total = jnp.where(receives, donor, jnp.zeros_like(donor))
    else:
        total_ref, part_ref, out_ref, next_ref = refs
        more = donor + times(donor, part_ref[...])
        total = total_ref[...] + jnp.where(receives, more, jnp.zeros_like(more))
    out_ref[...] = total
    next_ref[...] = (keep + donor + times(donor, matrix_ref[...])).astype(LOW)


def scan_end(forward, bit, position_ref, value_ref, other_ref, total_ref, part_ref):
    receives, donor, unused = scan_values(forward, bit, position_ref, value_ref, other_ref)
    times = dot if forward else dot_transposed
    more = donor + times(donor, part_ref[...])
    return total_ref[...] + jnp.where(receives, more, jnp.zeros_like(more))


def shards(token_ids, embedding, w_up, w_down, cotangent):
    depth = lax.axis_size("depth")
    bits = depth.bit_length() - 1
    assert depth == 1 << bits and bits >= 2
    position = lax.axis_index("depth")
    place = position.reshape(1).astype(jnp.int32)
    layers, width, inner_width = w_up.shape
    rows = token_ids.shape[0]
    layer_flops = 4 * rows * width * inner_width
    vocab_rows = embedding.shape[0]
    local_ids = token_ids - position * vocab_rows
    inside = (local_ids >= 0) & (local_ids < vocab_rows)
    picked = jnp.take(embedding, jnp.clip(local_ids, 0, vocab_rows - 1), axis=0)
    picked = jnp.where(inside[:, None], picked, jnp.zeros_like(picked))
    picked = picked + swapped(picked, "depth", 1)
    arrivals = [swapped(picked, "depth", mask) for mask in range(2, depth, 2)]
    for arrival in arrivals:
        picked = picked + arrival
    start = picked

    own = call(
        coarse_kernel,
        "coarse",
        4 * width * width * inner_width,
        12,
        shape((width, width), LOW),
        place,
        w_up,
        w_down,
    )
    steps = matrix_scan(own, place, bits)
    state_low = shape((rows, width), LOW)
    state_full = shape((rows, width), FULL)

    def forward_kernel(position_ref, start_ref, arrived_ref, up_ref, down_ref, out_ref):
        state = jnp.where(position_ref[0] == 0, start_ref[...], arrived_ref[...]).astype(FULL)
        out_ref[...] = block_forward(state, up_ref, down_ref).astype(LOW)

    def value_kernel(position_ref, start_ref, arrived_ref, own_ref, up_ref, down_ref, out_ref):
        state = jnp.where(position_ref[0] == 0, start_ref[...], arrived_ref[...]).astype(FULL)
        ended = block_forward(state, up_ref, down_ref)
        change = ended - state - dot(state, own_ref[...])
        out_ref[...] = jnp.where(position_ref[0] == 0, ended, change).astype(LOW)

    arrived = start
    for sweep in range(RELAX - 1):
        ended = call(
            forward_kernel,
            f"forward_{sweep}",
            layers * layer_flops,
            12,
            state_low,
            place,
            start,
            arrived,
            w_up,
            w_down,
        )
        arrived = rotated(ended, "depth", 1)
    value = call(
        value_kernel,
        "forward_value",
        layers * layer_flops,
        12,
        state_low,
        place,
        start,
        arrived,
        own,
        w_up,
        w_down,
    )

    def scanned(forward, value):
        total = None
        for bit in range(bits - 1):
            prefix, suffix, low, high = steps[bit]
            other = swapped(value, "depth", 1 << bit)
            args = (value, other, high if forward else low)
            if bit > 0:
                args = args + (total, prefix if forward else suffix)
            total, value = call(
                functools.partial(scan_kernel, forward, bit),
                f"scan_{int(forward)}_{bit}",
                4 * rows * width * width,
                8,
                [state_full, state_low],
                place,
                *args,
            )
        other = swapped(value, "depth", 1 << (bits - 1))
        prefix, suffix, unused, unused = steps[-1]
        return (value, other, total, prefix if forward else suffix)

    saved_shapes = lambda count: [
        shape((layers, count, inner_width), FULL),
        shape((layers, count, width), FULL),
        shape((layers, count, 1), FULL),
    ]

    def states_kernel(
        position_ref, value_ref, other_ref, total_ref, part_ref, start_ref, up_ref, down_ref,
        low_ref, slope_ref, unit_ref, scale_ref,
    ):
        corrected = scan_end(
            True, bits - 1, position_ref, value_ref, other_ref, total_ref, part_ref
        )
        corrected = jnp.where(position_ref[0] == 0, start_ref[...], corrected.astype(LOW))
        low_ref[...] = corrected
        save_forward(
            corrected.astype(FULL), up_ref, down_ref, slope_ref, unit_ref, scale_ref, None, None
        )

    corrected, slope, unit, scale = call(
        states_kernel,
        "states",
        layers * layer_flops,
        12,
        [state_low] + saved_shapes(rows),
        place,
        *scanned(True, value),
        start,
        w_up,
        w_down,
    )

    def adjoint_kernel(
        position_ref, final_ref, arrived_ref, slope_ref, unit_ref, scale_ref, up_ref, down_ref,
        out_ref,
    ):
        ends = position_ref[0] == depth - 1
        adjoint = jnp.where(ends, final_ref[...], arrived_ref[...]).astype(FULL)
        out_ref[...] = block_adjoint(
            adjoint, slope_ref, unit_ref, scale_ref, up_ref, down_ref
        ).astype(LOW)

    def adjoint_value_kernel(
        position_ref, final_ref, arrived_ref, own_ref, slope_ref, unit_ref, scale_ref, up_ref,
        down_ref, out_ref,
    ):
        ends = position_ref[0] == depth - 1
        adjoint = jnp.where(ends, final_ref[...], arrived_ref[...]).astype(FULL)
        begun = block_adjoint(adjoint, slope_ref, unit_ref, scale_ref, up_ref, down_ref)
        change = begun - adjoint - dot_transposed(adjoint, own_ref[...])
        out_ref[...] = jnp.where(ends, begun, change).astype(LOW)

    arrived = cotangent
    for sweep in range(RELAX - 1):
        begun = call(
            adjoint_kernel,
            f"adjoint_{sweep}",
            layers * layer_flops,
            12,
            state_low,
            place,
            cotangent,
            arrived,
            slope,
            unit,
            scale,
            w_up,
            w_down,
        )
        arrived = rotated(begun, "depth", -1)
    value = call(
        adjoint_value_kernel,
        "adjoint_value",
        layers * layer_flops,
        12,
        state_low,
        place,
        cotangent,
        arrived,
        own,
        slope,
        unit,
        scale,
        w_up,
        w_down,
    )

    def end_kernel(
        position_ref, value_ref, other_ref, total_ref, part_ref, final_ref, out_ref
    ):
        adjoint = scan_end(
            False, bits - 1, position_ref, value_ref, other_ref, total_ref, part_ref
        )
        ends = position_ref[0] == depth - 1
        out_ref[...] = jnp.where(ends, final_ref[...], adjoint.astype(LOW))

    adjoint = call(
        end_kernel,
        "scan_end",
        2 * rows * width * width,
        8,
        state_low,
        place,
        *scanned(False, value),
        cotangent,
    )

    parts = lax.axis_size("dp")
    part = lax.axis_index("dp")
    pieces = lambda block: [block] + [rotated(block, "dp", d) for d in range(1, parts)]
    corrected_pieces = pieces(corrected)
    adjoint_pieces = pieces(adjoint)

    def own_rows(block):
        size = block.shape[2] // parts
        return jnp.swapaxes(lax.dynamic_slice_in_dim(block, part * size, size, 2), 1, 2)

    def recompute_kernel(count, position_ref, *refs):
        state = jnp.concatenate([ref[...] for ref in refs[:count]], axis=0).astype(FULL)
        save_forward(state, *refs[count:])

    def grads_kernel(count, position_ref, *refs):
        adjoint = jnp.concatenate([ref[...] for ref in refs[:count]], axis=0).astype(FULL)
        slope_ref, unit_ref, scale_ref, normed_ref, hidden_ref = refs[count : count + 5]
        up_ref, down_ref, grad_up_ref, grad_down_ref = refs[count + 5 :]
        for layer in reversed(range(layers)):
            low = adjoint.astype(LOW)
            grad_down_ref[layer] = dot(hidden_ref[layer], low)
            toward_hidden = dot_transposed(low, down_ref[layer])
            delta = (toward_hidden * slope_ref[layer]).astype(LOW)
            grad_up_ref[layer] = dot(normed_ref[layer], delta)
            if layer > 0:
                toward_normed = dot_transposed(delta, up_ref[layer])
                unit = unit_ref[layer]
                inner = jnp.mean(toward_normed * unit, axis=-1, keepdims=True)
                adjoint = adjoint + scale_ref[layer] * (toward_normed - unit * inner)

    group = max(1, min(parts, CHUNK // rows))
    grads = None
    for begin in range(0, parts, group):
        chosen = slice(begin, min(begin + group, parts))
        count = len(range(parts)[chosen])
        tokens = count * rows
        inputs = corrected_pieces[chosen]
        if grads is not None:
            inputs, grads = lax.optimization_barrier((inputs, grads))
        slope, unit, scale, normed, hidden = call(
            functools.partial(recompute_kernel, count),
            f"recompute_{begin}",
            layers * layer_flops * count,
            24,
            saved_shapes(tokens)
            + [shape((layers, tokens, width), LOW), shape((layers, tokens, inner_width), LOW)],
            place,
            *inputs,
            w_up,
            w_down,
        )
        more = call(
            functools.partial(grads_kernel, count),
            f"grads_{begin}",
            layers * layer_flops * count,
            24,
            [
                shape((layers, width // parts, inner_width), FULL),
                shape((layers, inner_width // parts, width), FULL),
            ],
            place,
            *adjoint_pieces[chosen],
            slope,
            unit,
            scale,
            own_rows(normed),
            own_rows(hidden),
            w_up,
            w_down,
        )
        grads = more if grads is None else [a + b for a, b in zip(grads, more)]
    return tuple(grads)


def solution(mesh):
    in_specs = (
        P("dp"),
        P("depth", None),
        P("depth", None, None),
        P("depth", None, None),
        P("dp", None),
    )
    out_specs = (P("depth", "dp", None), P("depth", "dp", None))
    return jax.shard_map(shards, mesh=mesh, in_specs=in_specs, out_specs=out_specs, check_vma=False)
```

```python
import functools

import jax
import jax.numpy as jnp
from jax import lax
from jax.experimental import pallas as pl
from jax.experimental.pallas import tpu as pltpu
from jax.sharding import PartitionSpec as P


RELAX = 3


EPSILON = 1e-06
GAMMA = 0.05
CHUNK = 512
MIB = 1 << 20

LOW = jnp.bfloat16
FULL = jnp.float32


def swapped(block, axis, mask):
    devices = range(lax.axis_size(axis))
    return lax.ppermute(block, axis, [(i, i ^ mask) for i in devices])


def rotated(block, axis, distance):
    size = lax.axis_size(axis)
    return lax.ppermute(block, axis, [(i, (i + distance) % size) for i in range(size)])


def dot(left, right):
    return jnp.dot(left.astype(LOW), right.astype(LOW), preferred_element_type=FULL)


def dot_transposed(left, right):
    return lax.dot_general(
        left.astype(LOW), right.astype(LOW), (((1,), (1,)), ((), ())), preferred_element_type=FULL
    )


def call(body, flops, limit, out_shapes, position, *args):
    whole = pl.BlockSpec(memory_space=pltpu.VMEM)
    moved = sum(a.size * a.dtype.itemsize for a in args)
    return pl.pallas_call(
        body,
        out_shape=out_shapes,
        in_specs=[pl.BlockSpec(memory_space=pltpu.SMEM)] + [whole] * len(args),
        out_specs=jax.tree.map(lambda unused: whole, out_shapes),
        compiler_params=pltpu.CompilerParams(vmem_limit_bytes=limit * MIB),
        cost_estimate=pl.CostEstimate(flops=flops, bytes_accessed=moved // 4, transcendentals=0),
    )(position, *args)


def shape(dims, kind):
    return jax.ShapeDtypeStruct(dims, kind)


def row_scale(state):
    return lax.rsqrt(jnp.mean(state * state, axis=-1, keepdims=True) + EPSILON)


def block_forward(state, up_ref, down_ref):
    for layer in range(up_ref.shape[0]):
        normed = (state * row_scale(state)).astype(LOW)
        before = dot(normed, up_ref[layer])
        hidden = (before / (1.0 + jnp.exp(-before))).astype(LOW)
        state = state + dot(hidden, down_ref[layer])
    return state


def block_adjoint(adjoint, slope_ref, unit_ref, scale_ref, up_ref, down_ref):
    for layer in reversed(range(up_ref.shape[0])):
        toward_hidden = dot_transposed(adjoint, down_ref[layer])
        delta = (toward_hidden * slope_ref[layer]).astype(LOW)
        toward_normed = dot_transposed(delta, up_ref[layer])
        unit = unit_ref[layer]
        inner = jnp.mean(toward_normed * unit, axis=-1, keepdims=True)
        adjoint = adjoint + scale_ref[layer] * (toward_normed - unit * inner)
    return adjoint


def save_forward(state, up_ref, down_ref, slope_ref, unit_ref, scale_ref, keep=None):
    layers = up_ref.shape[0]
    for layer in range(layers):
        scale = row_scale(state)
        unit = state * scale
        normed = unit.astype(LOW)
        before = dot(normed, up_ref[layer])
        sigma = 1.0 / (1.0 + jnp.exp(-before))
        slope_ref[layer] = sigma * (1.0 + before * (1.0 - sigma))
        unit_ref[layer] = unit
        scale_ref[layer] = scale
        if keep is not None or layer < layers - 1:
            hidden = (before * sigma).astype(LOW)
            if keep is not None:
                keep(layer, normed, hidden)
            if layer < layers - 1:
                state = state + dot(hidden, down_ref[layer])


def own_columns(values, part, count):
    dims = (count, values.shape[1])
    columns = lax.broadcasted_iota(jnp.int32, dims, 1)
    chosen = lax.broadcasted_iota(jnp.int32, dims, 0) + part * count
    return dot_transposed((columns == chosen).astype(LOW), values).astype(LOW)


def coarse_kernel(position_ref, up_ref, down_ref, out_ref):
    total = dot(up_ref[0], down_ref[0])
    for layer in range(1, up_ref.shape[0]):
        total = total + dot(up_ref[layer], down_ref[layer])
    out_ref[...] = (GAMMA * total).astype(LOW)


def joined(left, right):
    return left.astype(FULL) + right.astype(FULL) + dot(left, right)


def join_kernel(bit, last, position_ref, whole_ref, *refs):
    upper = ((position_ref[0] >> bit) & 1) == 1
    odd = (position_ref[0] & 1) == 1
    refs = list(refs)
    whole = whole_ref[...]
    half = whole.shape[0] // 2
    if bit > 0:
        near, far = refs.pop(0)[...], refs.pop(0)[...]
        other = jnp.concatenate([jnp.where(odd, far, near), jnp.where(odd, near, far)], axis=0)
    else:
        other = refs.pop(0)[...]
    low = jnp.where(upper, other, whole)
    high = jnp.where(upper, whole, other)
    zeros = jnp.zeros_like(low)
    if bit > 0:
        before, after = refs.pop(0)[...], refs.pop(0)[...]
        prefix = jnp.where(upper, joined(low, before).astype(LOW), before)
        suffix = jnp.where(upper, after, joined(after, high).astype(LOW))
    else:
        prefix = jnp.where(upper, low, zeros)
        suffix = jnp.where(upper, zeros, high)
    refs[0][...] = low
    refs[1][...] = high
    refs[2][...] = prefix
    refs[3][...] = suffix
    if not last:
        both = joined(low, high).astype(LOW)
        refs[4][...] = both
        refs[5][...] = jnp.where(odd, both[half:], both[:half])


def matrix_scan(own, position, bits):
    width = own.shape[0]
    square = shape(own.shape, LOW)
    half = shape((width // 2, width), LOW)
    whole, part, prefix, suffix = own, None, None, None
    steps = []
    for bit in range(bits - 1):
        last = bit == bits - 2
        if bit == 0:
            args = (whole, swapped(whole, "depth", 1))
        else:
            near = swapped(part, "depth", 1 << bit)
            args = (whole, near, swapped(near, "depth", 1), prefix, suffix)
        outs = call(
            functools.partial(join_kernel, bit, last),
            6 * width**3,
            12,
            [square] * 4 + ([] if last else [square, half]),
            position,
            *args,
        )
        steps.append((prefix, suffix, outs[0], outs[1]))
        prefix, suffix = outs[2], outs[3]
        whole, part = (None, None) if last else outs[4:]
    steps.append((prefix, suffix, None, None))
    return steps


def scan_values(forward, bit, position_ref, value_ref, other_ref):
    upper = ((position_ref[0] >> bit) & 1) == 1
    value, other = value_ref[...].astype(FULL), other_ref[...].astype(FULL)
    lower_value = jnp.where(upper, other, value)
    upper_value = jnp.where(upper, value, other)
    if forward:
        return upper, lower_value, upper_value
    return jnp.logical_not(upper), upper_value, lower_value


def scan_kernel(forward, bit, position_ref, value_ref, other_ref, matrix_ref, *refs):
    receives, donor, keep = scan_values(forward, bit, position_ref, value_ref, other_ref)
    times = dot if forward else dot_transposed
    if bit == 0:
        out_ref, next_ref = refs
        total = jnp.where(receives, donor, jnp.zeros_like(donor))
    else:
        total_ref, part_ref, out_ref, next_ref = refs
        more = donor + times(donor, part_ref[...])
        total = total_ref[...] + jnp.where(receives, more, jnp.zeros_like(more))
    out_ref[...] = total
    next_ref[...] = (keep + donor + times(donor, matrix_ref[...])).astype(LOW)


def scan_end(forward, bit, position_ref, value_ref, other_ref, total_ref, part_ref):
    receives, donor, _ = scan_values(forward, bit, position_ref, value_ref, other_ref)
    times = dot if forward else dot_transposed
    more = donor + times(donor, part_ref[...])
    return total_ref[...] + jnp.where(receives, more, jnp.zeros_like(more))


def block_pass(token_ids, embedding, w_up, w_down, cotangent):
    depth = lax.axis_size("depth")
    bits = depth.bit_length() - 1
    assert depth == 1 << bits and bits >= 2
    position = lax.axis_index("depth")
    parts = lax.axis_size("dp")
    place = jnp.stack([position, lax.axis_index("dp")]).astype(jnp.int32)
    layers, width, inner_width = w_up.shape
    rows = token_ids.shape[0]
    layer_flops = 4 * rows * width * inner_width
    vocab_rows = embedding.shape[0]
    local_ids = token_ids - position * vocab_rows
    inside = (local_ids >= 0) & (local_ids < vocab_rows)
    picked = jnp.take(embedding, jnp.clip(local_ids, 0, vocab_rows - 1), axis=0)
    picked = jnp.where(inside[:, None], picked, jnp.zeros_like(picked))
    picked = picked + swapped(picked, "depth", 1)
    arrivals = []
    for mask in range(2, depth, 2):
        arrivals.append(swapped(picked, "depth", mask))
    for arrival in arrivals:
        picked = picked + arrival
    start = picked

    own = call(
        coarse_kernel,
        4 * width * width * inner_width,
        12,
        shape((width, width), LOW),
        place,
        w_up,
        w_down,
    )
    steps = matrix_scan(own, place, bits)
    state_low = shape((rows, width), LOW)
    state_full = shape((rows, width), FULL)

    def forward_kernel(position_ref, start_ref, arrived_ref, up_ref, down_ref, out_ref):
        state = jnp.where(position_ref[0] == 0, start_ref[...], arrived_ref[...]).astype(FULL)
        out_ref[...] = block_forward(state, up_ref, down_ref).astype(LOW)

    def value_kernel(position_ref, start_ref, arrived_ref, own_ref, up_ref, down_ref, out_ref):
        state = jnp.where(position_ref[0] == 0, start_ref[...], arrived_ref[...]).astype(FULL)
        ended = block_forward(state, up_ref, down_ref)
        change = ended - state - dot(state, own_ref[...])
        out_ref[...] = jnp.where(position_ref[0] == 0, ended, change).astype(LOW)

    arrived = start
    for _ in range(RELAX - 1):
        ended = call(
            forward_kernel, layers * layer_flops, 12, state_low, place, start, arrived, w_up, w_down
        )
        arrived = rotated(ended, "depth", 1)
    value = call(
        value_kernel, layers * layer_flops, 12, state_low, place, start, arrived, own, w_up, w_down
    )

    def scanned(forward, value):
        total = None
        for bit in range(bits - 1):
            prefix, suffix, low, high = steps[bit]
            other = swapped(value, "depth", 1 << bit)
            args = (value, other, high if forward else low)
            if bit > 0:
                args = args + (total, prefix if forward else suffix)
            total, value = call(
                functools.partial(scan_kernel, forward, bit),
                4 * rows * width * width,
                8,
                [state_full, state_low],
                place,
                *args,
            )
        other = swapped(value, "depth", 1 << (bits - 1))
        prefix, suffix, unused, unused = steps[-1]
        return (value, other, total, prefix if forward else suffix)

    saved_shapes = lambda count: [
        shape((layers, count, inner_width), FULL),
        shape((layers, count, width), FULL),
        shape((layers, count, 1), FULL),
    ]

    def states_kernel(
        position_ref, value_ref, other_ref, total_ref, part_ref, start_ref, up_ref, down_ref,
        low_ref, slope_ref, unit_ref, scale_ref,
    ):
        corrected = scan_end(
            True, bits - 1, position_ref, value_ref, other_ref, total_ref, part_ref
        )
        corrected = jnp.where(position_ref[0] == 0, start_ref[...], corrected.astype(LOW))
        low_ref[...] = corrected
        save_forward(
            corrected.astype(FULL), up_ref, down_ref, slope_ref, unit_ref, scale_ref
        )

    corrected, slope, unit, scale = call(
        states_kernel,
        layers * layer_flops,
        12,
        [state_low] + saved_shapes(rows),
        place,
        *scanned(True, value),
        start,
        w_up,
        w_down,
    )

    def adjoint_kernel(
        position_ref, final_ref, arrived_ref, slope_ref, unit_ref, scale_ref, up_ref, down_ref,
        out_ref,
    ):
        ends = position_ref[0] == depth - 1
        adjoint = jnp.where(ends, final_ref[...], arrived_ref[...]).astype(FULL)
        out_ref[...] = block_adjoint(
            adjoint, slope_ref, unit_ref, scale_ref, up_ref, down_ref
        ).astype(LOW)

    def adjoint_value_kernel(
        position_ref, final_ref, arrived_ref, own_ref, slope_ref, unit_ref, scale_ref, up_ref,
        down_ref, out_ref,
    ):
        ends = position_ref[0] == depth - 1
        adjoint = jnp.where(ends, final_ref[...], arrived_ref[...]).astype(FULL)
        begun = block_adjoint(adjoint, slope_ref, unit_ref, scale_ref, up_ref, down_ref)
        change = begun - adjoint - dot_transposed(adjoint, own_ref[...])
        out_ref[...] = jnp.where(ends, begun, change).astype(LOW)

    pieces = lambda block: [block] + [rotated(block, "dp", d) for d in range(1, parts)]
    arrived = cotangent
    for sweep in range(RELAX - 1):
        begun = call(
            adjoint_kernel,
            layers * layer_flops,
            12,
            state_low,
            place,
            cotangent,
            arrived,
            slope,
            unit,
            scale,
            w_up,
            w_down,
        )
        if sweep == 0:
            begun, corrected = lax.optimization_barrier((begun, corrected))
            corrected_pieces = pieces(corrected)
        arrived = rotated(begun, "depth", -1)
    arrived, corrected_pieces = lax.optimization_barrier((arrived, corrected_pieces))
    value = call(
        adjoint_value_kernel,
        layers * layer_flops,
        12,
        state_low,
        place,
        cotangent,
        arrived,
        own,
        slope,
        unit,
        scale,
        w_up,
        w_down,
    )

    def end_kernel(
        position_ref, value_ref, other_ref, total_ref, part_ref, final_ref, out_ref
    ):
        adjoint = scan_end(
            False, bits - 1, position_ref, value_ref, other_ref, total_ref, part_ref
        )
        ends = position_ref[0] == depth - 1
        out_ref[...] = jnp.where(ends, final_ref[...], adjoint.astype(LOW))

    adjoint = call(
        end_kernel, 2 * rows * width * width, 8, state_low, place, *scanned(False, value), cotangent
    )

    corrected_pieces, adjoint = lax.optimization_barrier((corrected_pieces, adjoint))
    adjoint_pieces = pieces(adjoint)

    def recompute_kernel(count, position_ref, *refs):
        state = jnp.concatenate([ref[...] for ref in refs[:count]], axis=0).astype(FULL)
        normed_ref, hidden_ref = refs[-2:]

        def keep(layer, normed, hidden):
            normed_ref[layer] = own_columns(normed, position_ref[1], width // parts)
            hidden_ref[layer] = own_columns(hidden, position_ref[1], inner_width // parts)

        save_forward(state, *refs[count:-2], keep)

    def grads_kernel(count, position_ref, *refs):
        adjoint = jnp.concatenate([ref[...] for ref in refs[:count]], axis=0).astype(FULL)
        slope_ref, unit_ref, scale_ref, normed_ref, hidden_ref = refs[count : count + 5]
        up_ref, down_ref, grad_up_ref, grad_down_ref = refs[count + 5 :]
        for layer in reversed(range(layers)):
            low = adjoint.astype(LOW)
            grad_down_ref[layer] = dot(hidden_ref[layer], low)
            toward_hidden = dot_transposed(low, down_ref[layer])
            delta = (toward_hidden * slope_ref[layer]).astype(LOW)
            grad_up_ref[layer] = dot(normed_ref[layer], delta)
            if layer > 0:
                toward_normed = dot_transposed(delta, up_ref[layer])
                unit = unit_ref[layer]
                inner = jnp.mean(toward_normed * unit, axis=-1, keepdims=True)
                adjoint = adjoint + scale_ref[layer] * (toward_normed - unit * inner)

    group = max(1, min(parts, CHUNK // rows))
    grads = None
    for begin in range(0, parts, group):
        chosen = slice(begin, min(begin + group, parts))
        count = len(range(parts)[chosen])
        tokens = count * rows
        inputs = corrected_pieces[chosen]
        if grads is not None:
            inputs, grads = lax.optimization_barrier((inputs, grads))
        slope, unit, scale, normed, hidden = call(
            functools.partial(recompute_kernel, count),
            layers * layer_flops * count,
            24,
            saved_shapes(tokens)
            + [
                shape((layers, width // parts, tokens), LOW),
                shape((layers, inner_width // parts, tokens), LOW),
            ],
            place,
            *inputs,
            w_up,
            w_down,
        )
        more = call(
            functools.partial(grads_kernel, count),
            layers * layer_flops * count,
            24,
            [
                shape((layers, width // parts, inner_width), FULL),
                shape((layers, inner_width // parts, width), FULL),
            ],
            place,
            *adjoint_pieces[chosen],
            slope,
            unit,
            scale,
            normed,
            hidden,
            w_up,
            w_down,
        )
        grads = more if grads is None else [a + b for a, b in zip(grads, more)]
    return tuple(grads)


def solution(mesh):
    in_specs = (
        P("dp"),
        P("depth", None),
        P("depth", None, None),
        P("depth", None, None),
        P("dp", None),
    )
    out_specs = (P("depth", "dp", None), P("depth", "dp", None))
    return jax.shard_map(block_pass, mesh=mesh, in_specs=in_specs, out_specs=out_specs, check_vma=False)
```

```python
import functools

import jax
import jax.numpy as jnp
from jax import lax
from jax.experimental import pallas as pl
from jax.experimental.pallas import tpu as pltpu
from jax.sharding import PartitionSpec as P


RELAX = 3


EPSILON = 1e-06
GAMMA = 0.05
CHUNK = 512
COARSE_STEPS = 2
LARGE = 44 << 20
MIB = 1 << 20

LOW = jnp.bfloat16
FULL = jnp.float32


def swapped(block, axis, mask):
    devices = range(lax.axis_size(axis))
    return lax.ppermute(block, axis, [(i, i ^ mask) for i in devices])


def rotated(block, axis, distance):
    size = lax.axis_size(axis)
    return lax.ppermute(block, axis, [(i, (i + distance) % size) for i in range(size)])


def dot(left, right):
    return jnp.dot(left.astype(LOW), right.astype(LOW), preferred_element_type=FULL)


def dot_transposed(left, right):
    return lax.dot_general(
        left.astype(LOW), right.astype(LOW), (((1,), (1,)), ((), ())), preferred_element_type=FULL
    )


def call(body, flops, limit, out_shapes, *args, scratch=()):
    whole = pl.BlockSpec(memory_space=pltpu.VMEM)
    moved = sum(a.size * a.dtype.itemsize for a in args)
    return pl.pallas_call(
        body,
        out_shape=out_shapes,
        in_specs=[whole] * len(args),
        out_specs=jax.tree.map(
            lambda unused: pl.BlockSpec(memory_space=pl.ANY) if scratch else whole, out_shapes
        ),
        scratch_shapes=list(scratch),
        compiler_params=pltpu.CompilerParams(vmem_limit_bytes=limit * MIB),
        cost_estimate=pl.CostEstimate(flops=flops, bytes_accessed=moved // 4, transcendentals=0),
    )(*args)


def shape(dims, kind):
    return jax.ShapeDtypeStruct(dims, kind)


def row_scale(state):
    return lax.rsqrt(jnp.mean(state * state, axis=-1, keepdims=True) + EPSILON)


def block_forward(state, up_ref, down_ref):
    for layer in range(up_ref.shape[0]):
        normed = (state * row_scale(state)).astype(LOW)
        before = dot(normed, up_ref[layer])
        hidden = (before / (1.0 + jnp.exp(-before))).astype(LOW)
        state = state + dot(hidden, down_ref[layer])
    return state


def block_adjoint(adjoint, slope_ref, unit_ref, scale_ref, up_ref, down_ref):
    for layer in reversed(range(up_ref.shape[0])):
        toward_hidden = dot(adjoint, down_ref[layer])
        delta = (toward_hidden * slope_ref[layer]).astype(LOW)
        toward_normed = dot(delta, up_ref[layer])
        unit = unit_ref[layer]
        inner = jnp.mean(toward_normed * unit, axis=-1, keepdims=True)
        adjoint = adjoint + scale_ref[layer] * (toward_normed - unit * inner)
    return adjoint


def save_forward(state, up_ref, down_ref, slope_ref, unit_ref, scale_ref, keep=None):
    layers = up_ref.shape[0]
    for layer in range(layers):
        scale = row_scale(state)
        unit = state * scale
        normed = unit.astype(LOW)
        before = dot(normed, up_ref[layer])
        sigma = 1.0 / (1.0 + jnp.exp(-before))
        slope_ref[layer] = sigma * (1.0 + before * (1.0 - sigma))
        unit_ref[layer] = unit
        scale_ref[layer] = scale
        if keep is not None or layer < layers - 1:
            hidden = (before * sigma).astype(LOW)
            if keep is not None:
                keep(layer, normed, hidden)
            if layer < layers - 1:
                state = state + dot(hidden, down_ref[layer])


def own_columns(values, part, count):
    dims = (count, values.shape[1])
    columns = lax.broadcasted_iota(jnp.int32, dims, 1)
    chosen = lax.broadcasted_iota(jnp.int32, dims, 0) + part * count
    return dot_transposed((columns == chosen).astype(LOW), values).astype(LOW)


def sum_kernel(*refs):
    total = refs[0][...]
    for ref in refs[1:-1]:
        total = total + ref[...]
    refs[-1][...] = total


def turn_kernel(in_ref, out_ref):
    for layer in range(in_ref.shape[0]):
        out_ref[layer] = in_ref[layer].T


def coarse_kernel(up_hbm, down_hbm, out_ref, up_ref, down_ref, sems):
    layers, _, inner = up_ref.shape
    step = inner // COARSE_STEPS
    copies = []
    for layer in range(layers):
        for begin in range(0, inner, step):
            for source, target in (
                (up_hbm.at[layer, :, pl.ds(begin, step)], up_ref.at[layer, :, pl.ds(begin, step)]),
                (down_hbm.at[layer, pl.ds(begin, step)], down_ref.at[layer, pl.ds(begin, step)]),
            ):
                copies.append(pltpu.make_async_copy(source, target, sems.at[len(copies)]))
                copies[-1].start()
    total = None
    for layer in range(layers):
        for begin in range(0, inner, step):
            copies.pop(0).wait()
            copies.pop(0).wait()
            more = dot(
                up_ref[layer, :, begin : begin + step], down_ref[layer, begin : begin + step]
            )
            total = more if total is None else total + more
    out_ref[...] = (GAMMA * total).astype(LOW)


def joined(left, right):
    return left.astype(FULL) + right.astype(FULL) + dot(left, right)


def join_kernel(bit, last, whole_ref, *refs):
    upper = ((lax.axis_index("depth") >> bit) & 1) == 1
    odd = (lax.axis_index("depth") & 1) == 1
    refs = list(refs)
    whole = whole_ref[...]
    half = whole.shape[0] // 2
    if bit > 0:
        near, far = refs.pop(0)[...], refs.pop(0)[...]
        other = jnp.concatenate([jnp.where(odd, far, near), jnp.where(odd, near, far)], axis=0)
    else:
        other = refs.pop(0)[...]
    low = jnp.where(upper, other, whole)
    high = jnp.where(upper, whole, other)
    zeros = jnp.zeros_like(low)
    if bit > 0:
        before, after = refs.pop(0)[...], refs.pop(0)[...]
        prefix = jnp.where(upper, joined(low, before).astype(LOW), before)
        suffix = jnp.where(upper, after, joined(after, high).astype(LOW))
    else:
        prefix = jnp.where(upper, low, zeros)
        suffix = jnp.where(upper, zeros, high)
    refs[0][...] = low
    refs[1][...] = high
    refs[2][...] = prefix
    refs[3][...] = suffix
    if not last:
        both = joined(low, high).astype(LOW)
        refs[4][...] = both
        refs[5][...] = jnp.where(odd, both[half:], both[:half])


def matrix_scan(own, bits):
    width = own.shape[0]
    square = shape(own.shape, LOW)
    half = shape((width // 2, width), LOW)
    whole, part, prefix, suffix = own, None, None, None
    steps = []
    for bit in range(bits - 1):
        last = bit == bits - 2
        if bit == 0:
            args = (whole, swapped(whole, "depth", 1))
        else:
            near = swapped(part, "depth", 1 << bit)
            args = (whole, near, swapped(near, "depth", 1), prefix, suffix)
        outs = call(
            functools.partial(join_kernel, bit, last),
            6 * width**3,
            12,
            [square] * 4 + ([] if last else [square, half]),
            *args,
        )
        steps.append((prefix, suffix, outs[0], outs[1]))
        prefix, suffix = outs[2], outs[3]
        whole, part = (None, None) if last else outs[4:]
    steps.append((prefix, suffix, None, None))
    return steps


def scan_values(forward, bit, value_ref, other_ref):
    upper = ((lax.axis_index("depth") >> bit) & 1) == 1
    value, other = value_ref[...].astype(FULL), other_ref[...].astype(FULL)
    lower_value = jnp.where(upper, other, value)
    upper_value = jnp.where(upper, value, other)
    if forward:
        return upper, lower_value, upper_value
    return jnp.logical_not(upper), upper_value, lower_value


def scan_kernel(forward, bit, value_ref, other_ref, matrix_ref, *refs):
    receives, donor, keep = scan_values(forward, bit, value_ref, other_ref)
    times = dot if forward else dot_transposed
    if bit == 0:
        out_ref, next_ref = refs
        total = jnp.where(receives, donor, jnp.zeros_like(donor))
    else:
        total_ref, part_ref, out_ref, next_ref = refs
        more = donor + times(donor, part_ref[...])
        total = total_ref[...] + jnp.where(receives, more, jnp.zeros_like(more))
    out_ref[...] = total
    next_ref[...] = (keep + donor + times(donor, matrix_ref[...])).astype(LOW)


def scan_end(forward, bit, value_ref, other_ref, total_ref, part_ref):
    receives, donor, _ = scan_values(forward, bit, value_ref, other_ref)
    times = dot if forward else dot_transposed
    more = donor + times(donor, part_ref[...])
    return total_ref[...] + jnp.where(receives, more, jnp.zeros_like(more))


def block_pass(token_ids, embedding, w_up, w_down, cotangent):
    depth = lax.axis_size("depth")
    bits = depth.bit_length() - 1
    assert depth == 1 << bits and bits >= 2
    parts = lax.axis_size("dp")
    layers, width, inner_width = w_up.shape
    rows = token_ids.shape[0]
    layer_flops = 4 * rows * width * inner_width
    state_low = shape((rows, width), LOW)
    state_full = shape((rows, width), FULL)
    apart = pl.BlockSpec(memory_space=pltpu.HBM)
    vocab_rows = embedding.shape[0]
    local_ids = token_ids - lax.axis_index("depth") * vocab_rows
    inside = (local_ids >= 0) & (local_ids < vocab_rows)
    picked = jnp.take(embedding, jnp.clip(local_ids, 0, vocab_rows - 1), axis=0)
    picked = jnp.where(inside[:, None], picked, jnp.zeros_like(picked))
    picked = picked + swapped(picked, "depth", 1)
    arrivals = []
    for mask in range(2, depth, 2):
        arrivals.append(swapped(picked, "depth", mask))
    start = call(sum_kernel, rows * width, 8, state_low, picked, *arrivals)

    whole = pl.BlockSpec(memory_space=pltpu.VMEM)
    own, w_up, w_down = pl.pallas_call(
        coarse_kernel,
        out_shape=[shape((width, width), LOW), shape(w_up.shape, LOW), shape(w_down.shape, LOW)],
        in_specs=[apart, apart],
        out_specs=[whole] * 3,
        scratch_shapes=[pltpu.SemaphoreType.DMA((2 * layers * COARSE_STEPS,))],
        name="coarse",
        compiler_params=pltpu.CompilerParams(vmem_limit_bytes=LARGE),
        cost_estimate=pl.CostEstimate(
            flops=4 * width * width * inner_width, bytes_accessed=2 * MIB, transcendentals=0
        ),
    )(w_up, w_down)
    steps = matrix_scan(own, bits)

    def forward_kernel(start_ref, arrived_ref, up_ref, down_ref, out_ref):
        state = jnp.where(lax.axis_index("depth") == 0, start_ref[...], arrived_ref[...]).astype(FULL)
        out_ref[...] = block_forward(state, up_ref, down_ref).astype(LOW)

    turned = {}
    for name, weights in (("turn_up", w_up), ("turn_down", w_down)):
        turned_shape = (layers, weights.shape[2], weights.shape[1])
        turned[name] = call(turn_kernel, layer_flops, 12, shape(turned_shape, LOW), weights)
    up_turned, down_turned = turned["turn_up"], turned["turn_down"]

    def value_kernel(start_ref, arrived_ref, own_ref, up_ref, down_ref, out_ref):
        state = jnp.where(lax.axis_index("depth") == 0, start_ref[...], arrived_ref[...]).astype(FULL)
        ended = block_forward(state, up_ref, down_ref)
        change = ended - state - dot(state, own_ref[...])
        out_ref[...] = jnp.where(lax.axis_index("depth") == 0, ended, change).astype(LOW)

    arrived = start
    for _ in range(RELAX - 1):
        ended = call(
            forward_kernel, layers * layer_flops, 12, state_low, start, arrived, w_up, w_down
        )
        arrived = rotated(ended, "depth", 1)
    value = call(
        value_kernel, layers * layer_flops, 12, state_low, start, arrived, own, w_up, w_down
    )

    def scanned(forward, value):
        total = None
        for bit in range(bits - 1):
            prefix, suffix, low, high = steps[bit]
            other = swapped(value, "depth", 1 << bit)
            args = (value, other, high if forward else low)
            if bit > 0:
                args = args + (total, prefix if forward else suffix)
            total, value = call(
                functools.partial(scan_kernel, forward, bit),
                4 * rows * width * width,
                8,
                [state_full, state_low],
                    *args,
            )
        other = swapped(value, "depth", 1 << (bits - 1))
        prefix, suffix, unused, unused = steps[-1]
        return (value, other, total, prefix if forward else suffix)

    saved_shapes = lambda count: [
        shape((layers, count, inner_width), FULL),
        shape((layers, count, width), FULL),
        shape((layers, count, 1), FULL),
    ]

    def states_kernel(
        value_ref, other_ref, total_ref, part_ref, start_ref, up_ref, down_ref,
        low_ref, slope_ref, unit_ref, scale_ref,
    ):
        corrected = scan_end(
            True, bits - 1, value_ref, other_ref, total_ref, part_ref
        )
        corrected = jnp.where(lax.axis_index("depth") == 0, start_ref[...], corrected.astype(LOW))
        low_ref[...] = corrected
        save_forward(
            corrected.astype(FULL), up_ref, down_ref, slope_ref, unit_ref, scale_ref
        )

    corrected, slope, unit, scale = call(
        states_kernel,
        layers * layer_flops,
        12,
        [state_low] + saved_shapes(rows),
        *scanned(True, value),
        start,
        w_up,
        w_down,
    )

    def adjoint_kernel(
        final_ref, arrived_ref, slope_ref, unit_ref, scale_ref, up_ref, down_ref,
        out_ref,
    ):
        ends = lax.axis_index("depth") == depth - 1
        adjoint = jnp.where(ends, final_ref[...], arrived_ref[...]).astype(FULL)
        out_ref[...] = block_adjoint(
            adjoint, slope_ref, unit_ref, scale_ref, up_ref, down_ref
        ).astype(LOW)

    def adjoint_value_kernel(
        final_ref, arrived_ref, own_ref, slope_ref, unit_ref, scale_ref, up_ref,
        down_ref, out_ref,
    ):
        ends = lax.axis_index("depth") == depth - 1
        adjoint = jnp.where(ends, final_ref[...], arrived_ref[...]).astype(FULL)
        begun = block_adjoint(adjoint, slope_ref, unit_ref, scale_ref, up_ref, down_ref)
        change = begun - adjoint - dot_transposed(adjoint, own_ref[...])
        out_ref[...] = jnp.where(ends, begun, change).astype(LOW)


    def pieces(block):
        arrived = [block]
        for distance in range(1, parts):
            arrived.append(rotated(block, "dp", distance))
        return arrived

    arrived = cotangent
    for sweep in range(RELAX - 1):
        begun = call(
            adjoint_kernel,
            layers * layer_flops,
            12,
            state_low,
            cotangent,
            arrived,
            slope,
            unit,
            scale,
            up_turned,
            down_turned,
        )
        if sweep == 0:
            begun, corrected = lax.optimization_barrier((begun, corrected))
            corrected_pieces = pieces(corrected)
        arrived = rotated(begun, "depth", -1)
    value = call(
        adjoint_value_kernel,
        layers * layer_flops,
        12,
        state_low,
        cotangent,
        arrived,
        own,
        slope,
        unit,
        scale,
        up_turned,
        down_turned,
    )

    def end_kernel(
        value_ref, other_ref, total_ref, part_ref, final_ref, out_ref
    ):
        adjoint = scan_end(
            False, bits - 1, value_ref, other_ref, total_ref, part_ref
        )
        ends = lax.axis_index("depth") == depth - 1
        out_ref[...] = jnp.where(ends, final_ref[...], adjoint.astype(LOW))

    adjoint = call(
        end_kernel, 2 * rows * width * width, 8, state_low, *scanned(False, value), cotangent
    )

    corrected_pieces, adjoint = lax.optimization_barrier((corrected_pieces, adjoint))
    adjoint_pieces = pieces(adjoint)

    def recompute_kernel(count, *refs):
        state = jnp.concatenate([ref[...] for ref in refs[:count]], axis=0).astype(FULL)
        normed_ref, hidden_ref = refs[-2:]

        def keep(layer, normed, hidden):
            normed_ref[layer] = own_columns(normed, lax.axis_index("dp"), width // parts)
            hidden_ref[layer] = own_columns(hidden, lax.axis_index("dp"), inner_width // parts)

        save_forward(state, *refs[count:-2], keep)

    def grads_kernel(count, *refs):
        adjoint = jnp.concatenate([ref[...] for ref in refs[:count]], axis=0).astype(FULL)
        slope_ref, unit_ref, scale_ref, normed_ref, hidden_ref = refs[count : count + 5]
        up_ref, down_ref, grad_up_ref, grad_down_ref = refs[count + 5 : count + 9]
        up_scratch, down_scratch, sems = refs[count + 9 :]
        copies = []

        def put(scratch, out_ref, layer, value):
            scratch[layer] = value
            sem = sems.at[len(copies)]
            copies.append(pltpu.make_async_copy(scratch.at[layer], out_ref.at[layer], sem))
            copies[-1].start()

        for layer in reversed(range(layers)):
            low = adjoint.astype(LOW)
            put(down_scratch, grad_down_ref, layer, dot(hidden_ref[layer], low))
            toward_hidden = dot(low, down_ref[layer])
            delta = (toward_hidden * slope_ref[layer]).astype(LOW)
            put(up_scratch, grad_up_ref, layer, dot(normed_ref[layer], delta))
            if layer > 0:
                toward_normed = dot(delta, up_ref[layer])
                unit = unit_ref[layer]
                inner = jnp.mean(toward_normed * unit, axis=-1, keepdims=True)
                adjoint = adjoint + scale_ref[layer] * (toward_normed - unit * inner)
        for copy in copies:
            copy.wait()

    group = max(1, min(parts, CHUNK // rows))
    grads = None
    for begin in range(0, parts, group):
        chosen = slice(begin, min(begin + group, parts))
        count = len(range(parts)[chosen])
        tokens = count * rows
        inputs = corrected_pieces[chosen]
        if grads is not None:
            inputs, grads = lax.optimization_barrier((inputs, grads))
        slope, unit, scale, normed, hidden = call(
            functools.partial(recompute_kernel, count),
            layers * layer_flops * count,
            20,
            saved_shapes(tokens)
            + [
                shape((layers, width // parts, tokens), LOW),
                shape((layers, inner_width // parts, tokens), LOW),
            ],
            *inputs,
            w_up,
            w_down,
        )
        grad_shapes = [
            shape((layers, width // parts, inner_width), FULL),
            shape((layers, inner_width // parts, width), FULL),
        ]
        more = call(
            functools.partial(grads_kernel, count),
            layers * layer_flops * count,
            20,
            grad_shapes,
            *adjoint_pieces[chosen],
            slope,
            unit,
            scale,
            normed,
            hidden,
            up_turned,
            down_turned,
            scratch=[pltpu.VMEM(leaf.shape, leaf.dtype) for leaf in grad_shapes]
            + [pltpu.SemaphoreType.DMA((2 * layers,))],
        )
        grads = more if grads is None else [a + b for a, b in zip(grads, more)]
    return tuple(grads)


def solution(mesh):
    in_specs = (
        P("dp"),
        P("depth", None),
        P("depth", None, None),
        P("depth", None, None),
        P("dp", None),
    )
    out_specs = (P("depth", "dp", None), P("depth", "dp", None))
    return jax.shard_map(block_pass, mesh=mesh, in_specs=in_specs, out_specs=out_specs, check_vma=False)
```
